32 devices in a mesh: group: 2 (over y), row: 4 (over x, core), col: 4 (over z).
Axes of the slice: x: 2, y: 2, z: 4, core: 2. Of those that a mesh axis runs over, the one named last changes fastest.
Arguments:
- patches: bfloat16 [64, 64, 1280], P(('group', 'row'), 'col'), parts along dimension 0, may hold values from -6 to 6
- patch_gain: bfloat16 [1280], replicated, may hold values from 0.25 to 1.75
- patch_bias: bfloat16 [1280], replicated, may hold values from -3 to 3
- merger_up: bfloat16 [5120, 5120], P('col', 'row'), may hold values from -0.078125 to 0.078125
- merger_up_bias: bfloat16 [5120], P('row'), may hold values from -3 to 3
- merger_down: bfloat16 [5120, 8192], P('row', 'col')
- merger_down_bias: bfloat16 [8192], P('col'), may hold values from -1.796875 to 1.796875
- norm_gain: bfloat16 [8192], P('col'), may hold values from 0.25 to 1.75
- w_gate: bfloat16 [8192, 14784], P('col', 'row'), may hold values from -0.0625 to 0.0625
- w_up: bfloat16 [8192, 14784], P('col', 'row'), may hold values from -0.0625 to 0.0625
- hidden_cotangent: bfloat16 [1024, 14784], P(('group', 'col'), 'row'), parts along dimension 0, may hold values from -0.59765625 to 0.59765625
- placement: int32 [64], P('group'), parts along dimension 0, may hold values from 0 to 31, as said below
- patch_counts: int32 [64], P('group'), parts along dimension 0, may hold values from 4 to 64, as said below
Outputs:
- merger_up_grad: float32 [10240, 5120], P(('group', 'col'), 'row'), parts along dimension 0
- merger_up_bias_grad: float32 [10240], P(('group', 'row')), parts along dimension 0
- merger_down_grad: float32 [10240, 8192], P(('group', 'row'), 'col'), parts along dimension 0
- merger_down_bias_grad: float32 [16384], P(('group', 'col')), parts along dimension 0
The draws below stay inside these ranges and needn't reach their ends.
There are 2 independent parts, one for each index of `group`. The reference program is written for one: setup_inputs(seed, part) draws one part's arguments, and reference() takes and returns one part's arrays. A program takes and returns all parts, laid end to end along the dimension named above; an argument that names none is the same for every part. Nothing has to cross between parts.
Inputs may be any that keep to these rules, and one draw needn't show every extreme that they name: `placement`: A permutation of the images onto the sequence blocks. Block b lies on index b // 8 of row, and image i on index i // 8. The 8 images of one index of row fill at most 2 blocks of any one index of row, and exactly 2 for some pair of indices in every draw. Every count is a multiple of 4; image i's first patch_counts[i] // 4 merged slots are real and the others are padding; some image has exactly 64 patches in every draw.
All inputs are finite; a program needn't handle non-finite values.
Results may differ from the reference program's by a relative error of at most 0.034.
Values may be sent and summed in bfloat16 or wider, within the bound.
A program may use at most 192 MiB of HBM per device.

```python
import math
import jax
import jax.numpy as jnp
from jax import lax

D = 8192
PATCH_DIM = 1280
MH = 5120
FFW = 14784
BLK = 16
IMG_ROW = 8
PATCHES = 64
MDIM = 5120
IMAGES = 32
TOKENS = 512
N_ROW = 4
N_COL = 4


def draw_merger_down(key, part):
    key_base, key_scale = jax.random.split(key)
    base = jax.random.normal(key_base, (MH, D), jnp.float32)
    rise = math.log(20.0)
    column = jnp.arange(D, dtype=jnp.float32) / D
    jitter = jax.random.uniform(key_scale, (D,), jnp.float32, -0.5, 0.5)
    scale = jnp.exp(rise * (column - 0.5) + math.log(2.0) * jitter)
    return (base * (scale / math.sqrt(MH))[None, :]).astype(jnp.bfloat16)


def draw_placement(key, part):
    groups = IMAGES // IMG_ROW
    key_order, key_rest, key_turn, key_slot = jax.random.split(jax.random.fold_in(key, 11), 4)
    order = jax.random.permutation(key_order, groups)
    remaining = jax.random.permutation(key_rest, jnp.concatenate([order[1:], order[1:]]))
    shifts = jnp.concatenate([order[:1], order[:1], remaining[:IMG_ROW - 2]])
    turns = jax.vmap(lambda one_key: jax.random.permutation(one_key, IMG_ROW))(jax.random.split(key_turn, groups))
    slots = jax.vmap(lambda one_key: jax.random.permutation(one_key, IMG_ROW))(jax.random.split(key_slot, groups))
    image_ids = jnp.arange(IMAGES, dtype=jnp.int32)
    source = image_ids // IMG_ROW
    local = image_ids % IMG_ROW
    which = turns[source, local]
    target = (source + shifts[which]) % groups
    return (target * IMG_ROW + slots[target, which]).astype(jnp.int32)


def draw_patch_counts(key, part):
    key_count, key_full = jax.random.split(jax.random.fold_in(key, 23))
    merged = jax.random.randint(key_count, (IMAGES,), 1, BLK + 1)
    chosen = jax.random.randint(key_full, (), 0, IMAGES)
    merged = jnp.where(jnp.arange(IMAGES) == chosen, BLK, merged)
    return (4 * merged).astype(jnp.int32)


def steps_of(rng, extent, cuts, least, high):
    def one(dim, shards_of):
        draws = jax.random.uniform(jax.random.fold_in(jax.random.fold_in(rng, 6), dim), (shards_of,), jnp.float32, least / len(cuts), high / len(cuts))
        return jnp.repeat(jnp.exp(draws), extent[dim] // shards_of).reshape((-1,) + (1,) * (len(extent) - dim - 1))

    loudness = one(*cuts[0])
    for cut in cuts[1:]:
        loudness = loudness * one(*cut)
    return loudness


def normal_values(rng, dims, scale, reach, cuts=(), held_as=jnp.bfloat16):
    result = scale * jax.random.normal(rng, dims, jnp.float32)
    if cuts:
        result = result * steps_of(rng, dims, cuts, -0.22, 0.18)
    return jnp.clip(result, -reach, reach).astype(held_as)


def setup_inputs(seed: int = 0, part: int = 0) -> dict:
    key_list = jax.random.split(jax.random.key(seed), 14)
    part_splits = jax.random.split(jax.random.fold_in(key_list[13], part), 14)
    return {
        "patches": normal_values(part_splits[0], (IMAGES, PATCHES, PATCH_DIM), 1.0, 6.0, ((0, 4), (1, 4))),
        "patch_gain": jnp.clip(1.0 + 0.15 * jax.random.normal(key_list[1], (PATCH_DIM,), jnp.float32), 0.25, 1.75).astype(jnp.bfloat16),
        "patch_bias": normal_values(key_list[2], (PATCH_DIM,), 0.5, 3.0),
        "merger_up": normal_values(key_list[3], (MDIM, MH), MDIM ** -0.5, 0.078125, ((0, 4), (1, 4))),
        "merger_up_bias": normal_values(key_list[4], (MH,), 0.5, 3.0, ((0, 4),)),
        "merger_down": draw_merger_down(jax.random.fold_in(key_list[13], 71), part),
        "merger_down_bias": normal_values(key_list[6], (D,), 0.3, 1.796875, ((0, 4),)),
        "norm_gain": jnp.clip(1.0 + 0.15 * jax.random.normal(key_list[7], (D,), jnp.float32), 0.25, 1.75).astype(jnp.bfloat16),
        "w_gate": normal_values(key_list[8], (D, FFW), D ** -0.5, 0.0625, ((0, 4), (1, 4))),
        "w_up": normal_values(key_list[9], (D, FFW), D ** -0.5, 0.0625, ((0, 4), (1, 4))),
        "hidden_cotangent": normal_values(part_splits[10], (TOKENS, FFW), 0.1, 0.59765625, ((0, 4), (1, 4))),
        "placement": draw_placement(jax.random.fold_in(jax.random.fold_in(key_list[13], part), 71), part),
        "patch_counts": draw_patch_counts(jax.random.fold_in(jax.random.fold_in(key_list[13], part), 71), part),
    }


EPS_PATCH = 1e-06
EPS_NORM = 1e-06

def rounded(inputs):
    return lax.optimization_barrier(inputs.astype(jnp.bfloat16)).astype(jnp.float32)

def gelu_slope(inputs):
    cumulative = 0.5 * (1.0 + jax.scipy.special.erf(inputs / math.sqrt(2.0)))
    return cumulative + inputs * jnp.exp(-0.5 * inputs * inputs) / math.sqrt(2.0 * math.pi)

def blocked_product(factors, pieces):
    row_count = factors[0][0].shape[0]
    col_count = factors[0][1].shape[1]
    block_width = factors[0][0].shape[1] // pieces

    def step(running, block_index):
        offset = block_index * block_width
        block_term = jnp.zeros((row_count, col_count), jnp.float32)
        for left_side, right_side in factors:
            left_block = lax.dynamic_slice_in_dim(left_side, offset, block_width, 1)
            right_block = lax.dynamic_slice_in_dim(right_side, offset, block_width, 0)
            block_term = block_term + jnp.dot(left_block, right_block, preferred_element_type=jnp.float32)
        return (running + rounded(block_term), None)
    running, unused = lax.scan(step, jnp.zeros((row_count, col_count), jnp.float32), jnp.arange(pieces, dtype=jnp.int32))
    return running

def reference(patches, patch_gain, patch_bias, merger_up, merger_up_bias, merger_down, merger_down_bias, norm_gain, w_gate, w_up, hidden_cotangent, placement, patch_counts):
    values = patches.astype(jnp.float32)
    center = values - lax.optimization_barrier(jnp.mean(values, axis=-1, keepdims=True))
    spread = lax.optimization_barrier(jnp.mean(center * center, axis=-1, keepdims=True))
    normed_patches = (center * lax.rsqrt(spread + EPS_PATCH) * patch_gain.astype(jnp.float32) + patch_bias.astype(jnp.float32)).astype(jnp.bfloat16)
    image_tokens = normed_patches.reshape(IMAGES, BLK, MDIM)
    image_ids = jnp.arange(IMAGES, dtype=jnp.int32)
    hit_table = placement[:, None] == image_ids[None, :]
    source = lax.optimization_barrier(jnp.sum(jnp.where(hit_table, image_ids[:, None], 0), axis=0)).astype(jnp.int32)
    sequence = image_tokens[source].reshape(TOKENS, MDIM)
    block_fill = lax.optimization_barrier(jnp.sum(jnp.where(hit_table, (patch_counts // 4)[:, None], 0), axis=0)).astype(jnp.int32)
    position = jnp.arange(TOKENS, dtype=jnp.int32)
    valid_rows = position % BLK < block_fill[position // BLK]
    pre_act = blocked_product([(sequence, merger_up)], N_COL) + merger_up_bias.astype(jnp.float32)
    hidden_merge = jax.nn.gelu(pre_act, approximate=False).astype(jnp.bfloat16)
    merged_out = lax.optimization_barrier((blocked_product([(hidden_merge, merger_down)], N_ROW) + merger_down_bias.astype(jnp.float32)).astype(jnp.bfloat16))
    merged_f = merged_out.astype(jnp.float32)
    inv_rms = lax.rsqrt(lax.optimization_barrier(jnp.sum(merged_f * merged_f, axis=1)) / D + EPS_NORM)
    gain = norm_gain.astype(jnp.float32)
    normed = (merged_f * inv_rms[:, None] * gain).astype(jnp.bfloat16)
    gate_out = lax.optimization_barrier(blocked_product([(normed, w_gate)], N_COL).astype(jnp.bfloat16))
    up_out = lax.optimization_barrier(blocked_product([(normed, w_up)], N_COL).astype(jnp.bfloat16))
    gate_f = gate_out.astype(jnp.float32)
    up_f = up_out.astype(jnp.float32)
    cotangent = jnp.where(valid_rows[:, None], hidden_cotangent.astype(jnp.float32), 0.0)
    logistic = jax.nn.sigmoid(gate_f)
    grad_gate = (cotangent * up_f * logistic * (1.0 + gate_f * (1.0 - logistic))).astype(jnp.bfloat16)
    grad_up = (cotangent * gate_f * logistic).astype(jnp.bfloat16)
    grad_normed = blocked_product([(grad_gate, w_gate.T), (grad_up, w_up.T)], N_ROW)
    gained = gain * grad_normed
    inner = lax.optimization_barrier(jnp.sum(merged_f * gained, axis=1))
    grad_merged = lax.optimization_barrier((inv_rms[:, None] * gained - merged_f * (inv_rms * inv_rms * inv_rms / D * inner)[:, None]).astype(jnp.bfloat16))
    merger_down_grad = jnp.dot(hidden_merge.T, grad_merged, preferred_element_type=jnp.float32)
    merger_down_bias_grad = lax.optimization_barrier(jnp.sum(grad_merged.astype(jnp.float32), axis=0))
    grad_hidden = blocked_product([(grad_merged, merger_down.T)], N_COL)
    grad_pre = lax.optimization_barrier((grad_hidden * gelu_slope(pre_act)).astype(jnp.bfloat16))
    merger_up_grad = jnp.dot(sequence.T, grad_pre, preferred_element_type=jnp.float32)
    merger_up_bias_grad = lax.optimization_barrier(jnp.sum(grad_pre.astype(jnp.float32), axis=0))
    return (merger_up_grad, merger_up_bias_grad, merger_down_grad, merger_down_bias_grad)
```

```python
import functools
import math

import jax
import jax.numpy as jnp
from jax import lax
from jax.sharding import PartitionSpec as P

D = 8192
BLK = 16
IMG_ROW = 8


EPS_PATCH = 1e-06
EPS_NORM = 1e-06
CONTRACT_ROWS = (((0,), (0,)), ((), ()))
CONTRACT_COLS = (((1,), (1,)), ((), ()))


def gelu_slope(inputs):
    cumulative = 0.5 * (1.0 + jax.scipy.special.erf(inputs / math.sqrt(2.0)))
    return cumulative + inputs * jnp.exp(-0.5 * inputs * inputs) / math.sqrt(2.0 * math.pi)


def patch_tokens(patches, patch_gain, patch_bias):
    values = patches.astype(jnp.float32)
    center = values - jnp.mean(values, axis=-1, keepdims=True)
    spread = jnp.mean(center * center, axis=-1, keepdims=True)
    normed = center * lax.rsqrt(spread + EPS_PATCH) * patch_gain.astype(
        jnp.float32
    ) + patch_bias.astype(jnp.float32)
    image_count, patch_slots, patch_width = patches.shape
    return normed.astype(jnp.bfloat16).reshape(image_count, patch_slots // 4, 4 * patch_width)


def swiglu_grads(gate_out, up_out, cotangent):
    gate_f = gate_out.astype(jnp.float32)
    up_f = up_out.astype(jnp.float32)
    masked = cotangent.astype(jnp.float32)
    logistic = jax.nn.sigmoid(gate_f)
    grad_gate = (masked * up_f * logistic * (1.0 + gate_f * (1.0 - logistic))).astype(jnp.bfloat16)
    grad_up = (masked * gate_f * logistic).astype(jnp.bfloat16)
    return (grad_gate, grad_up)


def pack_plan(placement, patch_counts, tokens, n_row, n_col, cap):
    images = placement.shape[0]
    rows = tokens // n_col
    blocks = rows // BLK
    ids = jnp.arange(images, dtype=jnp.int32)
    cols = jnp.arange(n_col, dtype=jnp.int32)
    hit = placement[:, None] == ids[None, :]
    fill = jnp.sum(jnp.where(hit, (patch_counts // 4)[:, None], 0), axis=0)
    owner = ids // blocks
    before = (owner[:, None] == owner[None, :]) & (ids[None, :] < ids[:, None])
    start = jnp.sum(jnp.where(before, fill[None, :], 0), axis=1)
    count = jnp.sum(jnp.where(owner[None, :] == cols[:, None], fill[None, :], 0), axis=1)
    over = jnp.maximum(count - cap, 0)
    free = jnp.maximum(cap - count, 0)
    lower = cols[None, :] < cols[:, None]
    over_start = jnp.sum(jnp.where(lower, over[None, :], 0), axis=1)
    free_start = jnp.sum(jnp.where(lower, free[None, :], 0), axis=1)

    def spill_slot(number):
        inside = (number[..., None] >= free_start) & (number[..., None] < free_start + free)
        return jnp.sum(
            jnp.where(inside, cols * cap + count + number[..., None] - free_start, 0), axis=-1
        )

    place = jnp.arange(BLK, dtype=jnp.int32)
    rank = start[:, None] + place[None, :]
    real = place[None, :] < fill[:, None]
    owner_over = jnp.sum(jnp.where(owner[:, None] == cols[None, :], over_start[None, :], 0), axis=1)
    slot = jnp.where(
        rank < cap,
        owner[:, None] * cap + rank,
        spill_slot(owner_over[:, None] + rank - cap),
    )
    slot = jnp.where(real, slot, -1)
    rank = jnp.where(real, rank, -1)
    by_image = jnp.sum(jnp.where(hit[:, :, None], slot[None, :, :], 0), axis=1)
    extra = jnp.arange(rows - cap, dtype=jnp.int32)
    extra_slot = jnp.where(
        extra[None, :] < over[:, None], spill_slot(over_start[:, None] + extra[None, :]), -1
    )
    return slot.reshape(-1), rank.reshape(-1), by_image, extra_slot.reshape(-1)


def one_hot(slots, first, size):
    return (slots[None, :] - first == jnp.arange(size, dtype=jnp.int32)[:, None]).astype(
        jnp.bfloat16
    )


def pick(selection, values):
    return jnp.dot(selection, values, preferred_element_type=jnp.float32)


def packed_step(cap, sequence_in, operands):
    (
        merger_up,
        merger_up_bias,
        merger_down,
        merger_down_bias,
        norm_gain,
        w_gate,
        w_up,
        hidden_cotangent,
        placement,
        patch_counts,
    ) = operands
    n_row = lax.axis_size("row")
    n_col = lax.axis_size("col")
    row_index = lax.axis_index("row")
    col_index = lax.axis_index("col")
    tokens = sequence_in.shape[0]
    held = hidden_cotangent.shape[0]
    packed = cap * n_col
    rows_row = packed // n_row
    slot, rank, by_image, extra_slot = pack_plan(
        placement, patch_counts, tokens, n_row, n_col, cap
    )
    arrival = by_image.reshape(n_row, IMG_ROW, n_col, BLK // n_col)
    arrival = jnp.transpose(arrival, (0, 2, 1, 3)).reshape(-1)
    sequence = pick(one_hot(arrival, 0, packed), sequence_in).astype(jnp.bfloat16)
    slot_here = lax.dynamic_slice_in_dim(slot, col_index * held, held)
    cotangent = pick(one_hot(slot_here, col_index * cap, cap), hidden_cotangent)
    if cap < held:
        rank_here = lax.dynamic_slice_in_dim(rank, col_index * held, held)
        spilled = pick(one_hot(rank_here, cap, held - cap), hidden_cotangent).astype(jnp.bfloat16)
        spilled_all = lax.all_gather(spilled, "col", axis=0, tiled=True)
        cotangent = cotangent + pick(one_hot(extra_slot, col_index * cap, cap), spilled_all)
    cotangent = cotangent.astype(jnp.bfloat16)

    pre_act = lax.psum_scatter(
        pick(sequence, merger_up).astype(jnp.bfloat16), "col", scatter_dimension=0, tiled=True
    ).astype(jnp.float32) + merger_up_bias.astype(jnp.float32)
    hidden_one = jax.nn.gelu(pre_act, approximate=False).astype(jnp.bfloat16)
    hidden_all = lax.all_gather(hidden_one, "col", axis=0, tiled=True)
    merged_out = lax.optimization_barrier(
        (
            lax.psum_scatter(
                pick(hidden_all, merger_down).astype(jnp.bfloat16),
                "row",
                scatter_dimension=0,
                tiled=True,
            ).astype(jnp.float32)
            + merger_down_bias.astype(jnp.float32)
        ).astype(jnp.bfloat16)
    )

    def row_sums(part):
        spread = jnp.where(
            jnp.arange(n_row, dtype=jnp.int32)[:, None] == row_index, part[None, :], 0.0
        )
        return lax.psum(spread.reshape(-1), ("row", "col"))

    merged_f = merged_out.astype(jnp.float32)
    merged_all = lax.all_gather(merged_out, "row", axis=0, tiled=True).astype(jnp.float32)
    square_sums = row_sums(jnp.sum(merged_f * merged_f, axis=1))
    inv_rms = lax.rsqrt(square_sums / D + EPS_NORM)
    gain = norm_gain.astype(jnp.float32)
    normed_all = (merged_all * inv_rms[:, None] * gain).astype(jnp.bfloat16)

    def gate_sums(weight):
        return lax.psum_scatter(
            pick(normed_all, weight).astype(jnp.bfloat16), "col", scatter_dimension=0, tiled=True
        )

    gate_out = gate_sums(w_gate)
    up_out = gate_sums(w_up)
    grad_gate, grad_up = swiglu_grads(gate_out, up_out, cotangent)
    grad_gate_all = lax.all_gather(grad_gate, "col", axis=0, tiled=True)
    grad_up_all = lax.all_gather(grad_up, "col", axis=0, tiled=True)
    from_gate = lax.dot_general(
        grad_gate_all, w_gate, CONTRACT_COLS, preferred_element_type=jnp.float32
    )
    grad_normed = lax.psum_scatter(
        (
            from_gate
            + lax.dot_general(grad_up_all, w_up, CONTRACT_COLS, preferred_element_type=jnp.float32)
        ).astype(jnp.bfloat16),
        "row",
        scatter_dimension=0,
        tiled=True,
    )
    inner = row_sums(jnp.sum(merged_f * (gain * grad_normed.astype(jnp.float32)), axis=1))
    gained_all = gain * lax.all_gather(grad_normed, "row", axis=0, tiled=True).astype(jnp.float32)
    grad_merged_all = (
        inv_rms[:, None] * gained_all
        - merged_all * (inv_rms * inv_rms * inv_rms / D * inner)[:, None]
    ).astype(jnp.bfloat16)
    grad_hidden = lax.psum_scatter(
        lax.dot_general(
            grad_merged_all, merger_down, CONTRACT_COLS, preferred_element_type=jnp.float32
        ).astype(jnp.bfloat16),
        "col",
        scatter_dimension=0,
        tiled=True,
    ).astype(jnp.float32)
    merger_down_grad = lax.dot_general(
        hidden_all, grad_merged_all, CONTRACT_ROWS, preferred_element_type=jnp.float32
    )
    merger_down_bias_grad = jnp.sum(grad_merged_all, axis=0, dtype=jnp.float32)
    grad_pre = (grad_hidden * gelu_slope(pre_act)).astype(jnp.bfloat16)
    grad_pre_all = lax.all_gather(grad_pre, "col", axis=0, tiled=True)
    merger_up_grad = lax.dot_general(
        sequence, grad_pre_all, CONTRACT_ROWS, preferred_element_type=jnp.float32
    )
    merger_up_bias_grad = jnp.sum(grad_pre_all, axis=0, dtype=jnp.float32)
    return (merger_up_grad, merger_up_bias_grad, merger_down_grad, merger_down_bias_grad)


def shards(
    patches,
    patch_gain,
    patch_bias,
    merger_up,
    merger_up_bias,
    merger_down,
    merger_down_bias,
    norm_gain,
    w_gate,
    w_up,
    hidden_cotangent,
    placement,
    patch_counts,
):
    n_col = lax.axis_size("col")
    held = hidden_cotangent.shape[0]
    real_rows = lax.pmax(jnp.sum(patch_counts // 4), "group")
    caps = [held * 5 // 8, held * 3 // 4, held]
    branch = sum((real_rows > cap * n_col).astype(jnp.int32) for cap in caps[:-1])
    image_tokens = patch_tokens(patches, patch_gain, patch_bias)
    slot_count = image_tokens.shape[1]
    feat_width = image_tokens.shape[2] // n_col
    sending = image_tokens.reshape(IMG_ROW * slot_count, n_col, feat_width)
    sending = jnp.transpose(sending, (1, 0, 2))
    received = lax.all_to_all(sending, "col", split_axis=0, concat_axis=0, tiled=True)
    merged = received.reshape(n_col * IMG_ROW * slot_count, feat_width)
    gathered_in = lax.all_gather(merged, "row", axis=0, tiled=True)
    operands = (
        merger_up,
        merger_up_bias,
        merger_down,
        merger_down_bias,
        norm_gain,
        w_gate,
        w_up,
        hidden_cotangent,
        placement,
        patch_counts,
    )
    return lax.switch(
        branch, [functools.partial(packed_step, cap) for cap in caps], gathered_in, operands
    )


def solution(mesh):
    in_specs = (
        P(("group", "row"), "col", None),
        P(),
        P(),
        P("col", "row"),
        P("row"),
        P("row", "col"),
        P("col"),
        P("col"),
        P("col", "row"),
        P("col", "row"),
        P(("group", "col"), "row"),
        P("group"),
        P("group"),
    )
    out_specs = (
        P(("group", "col"), "row"),
        P(("group", "row")),
        P(("group", "row"), "col"),
        P(("group", "col")),
    )
    return jax.shard_map(shards, mesh=mesh, in_specs=in_specs, out_specs=out_specs, check_vma=False)
```

```python
import functools
import math

import jax
import jax.numpy as jnp
from jax import lax
from jax.sharding import PartitionSpec as P

D = 8192
BLK = 16
IMG_ROW = 8


EPS_PATCH = 1e-06
EPS_NORM = 1e-06
CONTRACT_ROWS = (((0,), (0,)), ((), ()))
CONTRACT_COLS = (((1,), (1,)), ((), ()))


def gelu_slope(inputs):
    cumulative = 0.5 * (1.0 + jax.scipy.special.erf(inputs / math.sqrt(2.0)))
    return cumulative + inputs * jnp.exp(-0.5 * inputs * inputs) / math.sqrt(2.0 * math.pi)


def patch_tokens(patches, patch_gain, patch_bias):
    values = patches.astype(jnp.float32)
    center = values - jnp.mean(values, axis=-1, keepdims=True)
    spread = jnp.mean(center * center, axis=-1, keepdims=True)
    normed = center * lax.rsqrt(spread + EPS_PATCH) * patch_gain.astype(
        jnp.float32
    ) + patch_bias.astype(jnp.float32)
    image_count, patch_slots, patch_width = patches.shape
    return normed.astype(jnp.bfloat16).reshape(image_count, patch_slots // 4, 4 * patch_width)


def swiglu_grads(gate_out, up_out, cotangent):
    gate_f = gate_out.astype(jnp.float32)
    up_f = up_out.astype(jnp.float32)
    masked = cotangent.astype(jnp.float32)
    logistic = jax.nn.sigmoid(gate_f)
    grad_gate = (masked * up_f * logistic * (1.0 + gate_f * (1.0 - logistic))).astype(jnp.bfloat16)
    grad_up = (masked * gate_f * logistic).astype(jnp.bfloat16)
    return (grad_gate, grad_up)


def pack_plan(placement, patch_counts, tokens, n_row, n_col, cap):
    images = placement.shape[0]
    rows = tokens // n_col
    blocks = rows // BLK
    ids = jnp.arange(images, dtype=jnp.int32)
    cols = jnp.arange(n_col, dtype=jnp.int32)
    hit = placement[:, None] == ids[None, :]
    fill = jnp.sum(jnp.where(hit, (patch_counts // 4)[:, None], 0), axis=0)
    owner = ids // blocks
    before = (owner[:, None] == owner[None, :]) & (ids[None, :] < ids[:, None])
    start = jnp.sum(jnp.where(before, fill[None, :], 0), axis=1)
    count = jnp.sum(jnp.where(owner[None, :] == cols[:, None], fill[None, :], 0), axis=1)
    over = jnp.maximum(count - cap, 0)
    free = jnp.maximum(cap - count, 0)
    lower = cols[None, :] < cols[:, None]
    over_start = jnp.sum(jnp.where(lower, over[None, :], 0), axis=1)
    free_start = jnp.sum(jnp.where(lower, free[None, :], 0), axis=1)

    def spill_slot(number):
        inside = (number[..., None] >= free_start) & (number[..., None] < free_start + free)
        return jnp.sum(
            jnp.where(inside, cols * cap + count + number[..., None] - free_start, 0), axis=-1
        )

    place = jnp.arange(BLK, dtype=jnp.int32)
    rank = start[:, None] + place[None, :]
    real = place[None, :] < fill[:, None]
    owner_over = jnp.sum(jnp.where(owner[:, None] == cols[None, :], over_start[None, :], 0), axis=1)
    slot = jnp.where(
        rank < cap,
        owner[:, None] * cap + rank,
        spill_slot(owner_over[:, None] + rank - cap),
    )
    slot = jnp.where(real, slot, -1)
    rank = jnp.where(real, rank, -1)
    by_image = jnp.sum(jnp.where(hit[:, :, None], slot[None, :, :], 0), axis=1)
    extra = jnp.arange(rows - cap, dtype=jnp.int32)
    extra_slot = jnp.where(
        extra[None, :] < over[:, None], spill_slot(over_start[:, None] + extra[None, :]), -1
    )
    return slot.reshape(-1), rank.reshape(-1), by_image, extra_slot.reshape(-1)


def one_hot(slots, first, size):
    return (slots[None, :] - first == jnp.arange(size, dtype=jnp.int32)[:, None]).astype(
        jnp.bfloat16
    )


def pick(selection, values):
    return jnp.dot(selection, values, preferred_element_type=jnp.float32)


def shift_by(values, axis, step):
    size = lax.axis_size(axis)
    return lax.ppermute(values, axis, [(i, (i + step) % size) for i in range(size)])


def sum_direct(part, axis):
    total = part
    for step in range(1, lax.axis_size(axis)):
        total = total + shift_by(part, axis, step)
    return total


def gather_small(part, axis):
    size = lax.axis_size(axis)
    index = lax.axis_index(axis)
    ids = jnp.arange(size, dtype=jnp.int32)[:, None]
    out = jnp.where(ids == index, part[None, :], 0.0)
    for step in range(1, size):
        came = shift_by(part, axis, step)
        out = jnp.where(ids == (index - step) % size, came[None, :], out)
    return out.reshape(-1)


def scatter_direct(partial, axis):
    size = lax.axis_size(axis)
    index = lax.axis_index(axis)
    rows = partial.shape[0] // size

    def piece(owner):
        return lax.dynamic_slice_in_dim(partial, owner * rows, rows)

    total = piece(index).astype(jnp.float32)
    for step in range(1, size):
        came = shift_by(piece((index + step) % size), axis, step)
        total = total + came.astype(jnp.float32)
    return total


def packed_step(cap, sequence_in, operands):
    (
        merger_up,
        merger_up_bias,
        merger_down,
        merger_down_bias,
        norm_gain,
        w_gate,
        w_up,
        hidden_cotangent,
        placement,
        patch_counts,
    ) = operands
    n_row = lax.axis_size("row")
    n_col = lax.axis_size("col")
    col_index = lax.axis_index("col")
    tokens = sequence_in.shape[0]
    held = hidden_cotangent.shape[0]
    packed = cap * n_col
    slot, rank, by_image, extra_slot = pack_plan(
        placement, patch_counts, tokens, n_row, n_col, cap
    )
    arrival = by_image.reshape(n_row, IMG_ROW, n_col, BLK // n_col)
    arrival = jnp.stack(
        [
            lax.dynamic_index_in_dim(arrival, (col_index - step) % n_col, axis=2, keepdims=False)
            for step in range(n_col)
        ],
        axis=1,
    ).reshape(-1)
    sequence = pick(one_hot(arrival, 0, packed), sequence_in).astype(jnp.bfloat16)
    slot_here = lax.dynamic_slice_in_dim(slot, col_index * held, held)
    cotangent = pick(one_hot(slot_here, col_index * cap, cap), hidden_cotangent)
    if cap < held:
        rank_here = lax.dynamic_slice_in_dim(rank, col_index * held, held)
        spilled = pick(one_hot(rank_here, cap, held - cap), hidden_cotangent).astype(jnp.bfloat16)
        spilled_all = lax.all_gather(spilled, "col", axis=0, tiled=True)
        cotangent = cotangent + pick(one_hot(extra_slot, col_index * cap, cap), spilled_all)
    cotangent = cotangent.astype(jnp.bfloat16)

    pre_act = lax.psum_scatter(
        pick(sequence, merger_up).astype(jnp.bfloat16), "col", scatter_dimension=0, tiled=True
    ).astype(jnp.float32) + merger_up_bias.astype(jnp.float32)
    hidden_one = jax.nn.gelu(pre_act, approximate=False).astype(jnp.bfloat16)
    hidden_all = lax.all_gather(hidden_one, "col", axis=0, tiled=True)
    merged_out = lax.optimization_barrier(
        (
            scatter_direct(pick(hidden_all, merger_down).astype(jnp.bfloat16), "row")
            + merger_down_bias.astype(jnp.float32)
        ).astype(jnp.bfloat16)
    )

    def row_sums(part):
        return gather_small(sum_direct(part, "col"), "row")

    merged_f = merged_out.astype(jnp.float32)
    merged_all = lax.all_gather(merged_out, "row", axis=0, tiled=True).astype(jnp.float32)
    square_sums = row_sums(jnp.sum(merged_f * merged_f, axis=1))
    inv_rms = lax.rsqrt(square_sums / D + EPS_NORM)
    gain = norm_gain.astype(jnp.float32)
    normed_all = lax.optimization_barrier(
        (merged_all * inv_rms[:, None] * gain).astype(jnp.bfloat16)
    )

    def block_sums(rows, weight):
        return lax.psum_scatter(
            pick(rows, weight).astype(jnp.bfloat16), "col", scatter_dimension=0, tiled=True
        )

    gate_out = block_sums(normed_all, w_gate)
    up_out = block_sums(normed_all, w_up)
    grad_gate, grad_up = swiglu_grads(gate_out, up_out, cotangent)
    grad_gate_all = lax.all_gather(grad_gate, "col", axis=0, tiled=True)
    grad_up_all = lax.all_gather(grad_up, "col", axis=0, tiled=True)
    from_gate = lax.dot_general(
        grad_gate_all, w_gate, CONTRACT_COLS, preferred_element_type=jnp.float32
    )
    from_up = lax.dot_general(
        grad_up_all, w_up, CONTRACT_COLS, preferred_element_type=jnp.float32
    )
    grad_normed = scatter_direct((from_gate + from_up).astype(jnp.bfloat16), "row").astype(
        jnp.bfloat16
    )
    inner = row_sums(jnp.sum(merged_f * (gain * grad_normed.astype(jnp.float32)), axis=1))
    gained_all = gain * lax.all_gather(grad_normed, "row", axis=0, tiled=True).astype(jnp.float32)
    grad_merged_all = (
        inv_rms[:, None] * gained_all
        - merged_all * (inv_rms * inv_rms * inv_rms / D * inner)[:, None]
    ).astype(jnp.bfloat16)
    grad_hidden = lax.psum_scatter(
        lax.dot_general(
            grad_merged_all, merger_down, CONTRACT_COLS, preferred_element_type=jnp.float32
        ).astype(jnp.bfloat16),
        "col",
        scatter_dimension=0,
        tiled=True,
    ).astype(jnp.float32)
    merger_down_grad = lax.dot_general(
        hidden_all, grad_merged_all, CONTRACT_ROWS, preferred_element_type=jnp.float32
    )
    merger_down_bias_grad = jnp.sum(grad_merged_all, axis=0, dtype=jnp.float32)
    grad_pre = (grad_hidden * gelu_slope(pre_act)).astype(jnp.bfloat16)
    grad_pre_all = lax.all_gather(grad_pre, "col", axis=0, tiled=True)
    merger_up_grad = lax.dot_general(
        sequence, grad_pre_all, CONTRACT_ROWS, preferred_element_type=jnp.float32
    )
    merger_up_bias_grad = jnp.sum(grad_pre_all, axis=0, dtype=jnp.float32)
    return (merger_up_grad, merger_up_bias_grad, merger_down_grad, merger_down_bias_grad)


def shards(
    patches,
    patch_gain,
    patch_bias,
    merger_up,
    merger_up_bias,
    merger_down,
    merger_down_bias,
    norm_gain,
    w_gate,
    w_up,
    hidden_cotangent,
    placement,
    patch_counts,
):
    n_col = lax.axis_size("col")
    held = hidden_cotangent.shape[0]
    own_rows = jnp.sum(patch_counts // 4)
    real_rows = own_rows
    for step in range(1, lax.axis_size("group")):
        real_rows = jnp.maximum(real_rows, shift_by(own_rows, "group", step))
    caps = [held * 5 // 8, held * 3 // 4, held]
    branch = sum((real_rows > cap * n_col).astype(jnp.int32) for cap in caps[:-1])
    image_tokens = patch_tokens(patches, patch_gain, patch_bias)
    slot_count = image_tokens.shape[1]
    feat_width = image_tokens.shape[2] // n_col
    sending = image_tokens.reshape(IMG_ROW * slot_count, n_col, feat_width)
    sending = jnp.transpose(sending, (1, 0, 2))
    col_index = lax.axis_index("col")
    pieces = [lax.dynamic_index_in_dim(sending, col_index, keepdims=False)]
    for step in range(1, n_col):
        outgoing = lax.dynamic_index_in_dim(
            sending, (col_index + step) % n_col, keepdims=False
        )
        pieces.append(shift_by(outgoing, "col", step))
    merged = jnp.concatenate(pieces, axis=0)
    gathered_in = lax.all_gather(merged, "row", axis=0, tiled=True)
    operands = (
        merger_up,
        merger_up_bias,
        merger_down,
        merger_down_bias,
        norm_gain,
        w_gate,
        w_up,
        hidden_cotangent,
        placement,
        patch_counts,
    )
    return lax.switch(
        branch, [functools.partial(packed_step, cap) for cap in caps], gathered_in, operands
    )


def solution(mesh):
    in_specs = (
        P(("group", "row"), "col", None),
        P(),
        P(),
        P("col", "row"),
        P("row"),
        P("row", "col"),
        P("col"),
        P("col"),
        P("col", "row"),
        P("col", "row"),
        P(("group", "col"), "row"),
        P("group"),
        P("group"),
    )
    out_specs = (
        P(("group", "col"), "row"),
        P(("group", "row")),
        P(("group", "row"), "col"),
        P(("group", "col")),
    )
    return jax.shard_map(shards, mesh=mesh, in_specs=in_specs, out_specs=out_specs, check_vma=False)
```
